32 devices in a mesh: nodes: 8 (over z, x), mp: 4 (over y, core).
Axes of the slice: x: 2, y: 2, z: 4, core: 2. Of those that a mesh axis runs over, the one named last changes fastest.
Arguments:
- grid_in: bfloat16 [8192, 1024], P('nodes', 'mp'), may hold values from -2200 to 2200
- mesh_in: bfloat16 [2048, 1024], P('nodes', 'mp'), may hold values from -2200 to 2200
- w_query: bfloat16 [4, 1024, 512], P(None, None, 'mp'), as said below
- w_key: bfloat16 [4, 1024, 512], P(None, None, 'mp'), may hold values from -8 to 8
- w_value: bfloat16 [4, 1024, 512], P(None, None, 'mp'), may hold values from -0.1875 to 0.1875
- w_out: bfloat16 [4, 512, 1024], P(None, 'mp'), may hold values from -1 to 1
- norm_gains: float32 [6, 1024], replicated, may hold values from 0.25 to 1.75
- enc_list: int32 [16, 4], P('nodes'), may hold values from 0 to 63, as said below
- proc_list: int32 [16, 3], P('nodes'), may hold values from 0 to 15, as said below
- dec_list: int32 [64, 2], P('nodes'), may hold values from 0 to 15, as said below
- grid_count: int32 [64], replicated, may hold values from 1 to 128
Outputs:
- grid_out: bfloat16 [8192, 1024], P('nodes', 'mp')
- mesh_out: bfloat16 [2048, 1024], P('nodes', 'mp')
The draws below stay inside these ranges and needn't reach their ends.
Inputs may be any that keep to these rules, and one draw needn't show every extreme that they name: `enc_list`: mesh block b lies with node index b // 2; its 4 entries are distinct grid blocks held by node indices at most 2 from it (grid block c lies with node index c // 8). `proc_list`: entry 0 of row b is b; the others are distinct mesh blocks other than b held by node indices at most 2 from b's. `dec_list`: grid block c's 2 entries are distinct mesh blocks held by node indices at most 2 from c's. `w_query`: entries within 6 / sqrt(1024) of zero.
All inputs are finite; a program needn't handle non-finite values.
Results may differ from the reference program's by a relative error of at most 0.019.
Values may be sent and summed in bfloat16 or wider, within the bound.
A program may use at most 64 MiB of HBM per device.

```python
import jax
import jax.numpy as jnp
from jax import lax

D = 1024
HEADS = 8
HEAD_DIM = 64
BLOCK = 128
REACH = 2
LIST_ENC = 4
LIST_PROC = 3
LIST_DEC = 2
GB_DEV = 8
MB_DEV = 2
HD = 512
GRID_BLOCKS = 64
MESH_BLOCKS = 16
N_MP = 4


def drawn_rows(key, row_count, salt):
    return jnp.clip(jax.random.normal(jax.random.fold_in(key, salt), (row_count, D)), -6.0, 6.0)


def draw_grid_in(key, part):
    states = drawn_rows(key, GRID_BLOCKS * BLOCK, 11)
    return states.astype(jnp.bfloat16)


def draw_mesh_in(key, part):
    states = drawn_rows(key, MESH_BLOCKS * BLOCK, 21)
    return states.astype(jnp.bfloat16)


def query_table(key):
    return jnp.clip(jax.random.normal(jax.random.fold_in(key, 31), (4, D, HEADS * HEAD_DIM)), -6.0, 6.0) * D ** (-0.5)


def draw_w_query(key, part):
    return query_table(key).astype(jnp.bfloat16)


def draw_w_key(key, part):
    noise = jnp.clip(jax.random.normal(jax.random.fold_in(key, 41), (4, D, HEADS * HEAD_DIM)), -6.0, 6.0) * D ** (-0.5)
    result = noise
    return result.astype(jnp.bfloat16)


def pick_window(key, query_blocks, per_query, per_key, key_total, count, skip_self):
    width_blocks = (2 * REACH + 1) * per_key
    device_of = jnp.arange(query_blocks) // per_query
    window_start = (device_of - REACH) * per_key
    positions = jnp.arange(width_blocks)
    candidate = window_start[:, None] + positions[None, :]
    usable = (candidate >= 0) & (candidate < key_total)
    if skip_self:
        usable = usable & (candidate != jnp.arange(query_blocks)[:, None])
    priority = jax.random.randint(key, (query_blocks, width_blocks), 0, 1 << 20) * width_blocks + positions[None, :]
    priority = jnp.where(usable, priority, -1 - positions[None, :])
    highest, places = lax.top_k(priority, count)
    return (window_start[:, None] + places).astype(jnp.int32)


def draw_enc_list(key, part):
    return pick_window(jax.random.fold_in(key, 51), MESH_BLOCKS, MB_DEV, GB_DEV, GRID_BLOCKS, LIST_ENC, False)


def draw_proc_list(key, part):
    others = pick_window(jax.random.fold_in(key, 52), MESH_BLOCKS, MB_DEV, MB_DEV, MESH_BLOCKS, LIST_PROC - 1, True)
    itself = jnp.arange(MESH_BLOCKS).astype(jnp.int32)[:, None]
    return jnp.concatenate([itself, others], axis=1).astype(jnp.int32)


def draw_dec_list(key, part):
    return pick_window(jax.random.fold_in(key, 53), GRID_BLOCKS, GB_DEV, MB_DEV, MESH_BLOCKS, LIST_DEC, False)


def with_ends(values, own_key, least, top_value):
    extent = values.shape
    place = [jax.random.randint(jax.random.fold_in(own_key, axis), (), 0, extent[axis]) for axis in range(len(extent))]
    values = values.at[tuple(place)].set(least)
    longest = extent.index(max(extent))
    place[longest] = (place[longest] + 1) % extent[longest]
    return values.at[tuple(place)].set(top_value)


def steps_of(own_key, extent, shards, smallest, high):
    def one(position, blocks):
        heights = jax.random.uniform(jax.random.fold_in(jax.random.fold_in(own_key, 6), position), (blocks,), jnp.float32, smallest / len(shards), high / len(shards))
        return jnp.repeat(jnp.exp(heights), extent[position] // blocks).reshape((-1,) + (1,) * (len(extent) - position - 1))

    factor_of = one(*shards[0])
    for cut in shards[1:]:
        factor_of = factor_of * one(*cut)
    return factor_of


def normal_values(own_key, extent, scale, bound, split=(), held_as=jnp.bfloat16):
    drawn = scale * jax.random.normal(own_key, extent, jnp.float32)
    if split:
        drawn = drawn * steps_of(own_key, extent, split, -0.22, 0.18)
    return jnp.clip(drawn, -bound, bound).astype(held_as)


def setup_inputs(seed: int = 0) -> dict:
    arg_keys = jax.random.split(jax.random.key(seed), 12)
    return {
        "grid_in": draw_grid_in(jax.random.fold_in(arg_keys[11], 71), 0),
        "mesh_in": draw_mesh_in(jax.random.fold_in(arg_keys[11], 71), 0),
        "w_query": draw_w_query(jax.random.fold_in(arg_keys[11], 71), 0),
        "w_key": draw_w_key(jax.random.fold_in(arg_keys[11], 71), 0),
        "w_value": normal_values(arg_keys[4], (4, D, HD), D ** -0.5, 0.1875, ((2, 4),)),
        "w_out": normal_values(arg_keys[5], (4, HD, D), (HD // 16) ** -0.5, 1.0, ((1, 4),)),
        "norm_gains": jnp.clip(1.0 + 0.15 * jax.random.normal(arg_keys[6], (6, D), jnp.float32), 0.25, 1.75),
        "enc_list": draw_enc_list(jax.random.fold_in(arg_keys[11], 71), 0),
        "proc_list": draw_proc_list(jax.random.fold_in(arg_keys[11], 71), 0),
        "dec_list": draw_dec_list(jax.random.fold_in(arg_keys[11], 71), 0),
        "grid_count": with_ends(jax.random.randint(arg_keys[10], (GRID_BLOCKS,), 1, BLOCK + 1), jax.random.fold_in(arg_keys[10], 1), 1, BLOCK).astype(jnp.int32),
    }


epsilon = 1e-05

def normalize(states, gains):
    values = states.astype(jnp.float32)
    average = lax.optimization_barrier(jnp.mean(values, axis=-1, keepdims=True))
    centred = values - average
    spread = lax.optimization_barrier(jnp.mean(centred * centred, axis=-1, keepdims=True))
    return (centred * lax.rsqrt(spread + epsilon) * gains).astype(jnp.bfloat16)

def project(inputs, weight):
    return jnp.dot(inputs, weight, preferred_element_type=jnp.float32).astype(jnp.bfloat16)

def attend(queries, key_rows, values, key_ok):
    batch_count, row_count, head_width = queries.shape
    key_count = key_rows.shape[1]
    head_count = head_width // HEAD_DIM
    query_heads = queries.reshape(batch_count, row_count, head_count, HEAD_DIM).astype(jnp.float32)
    key_heads = key_rows.reshape(batch_count, key_count, head_count, HEAD_DIM).astype(jnp.float32)
    value_heads = values.reshape(batch_count, key_count, head_count, HEAD_DIM).astype(jnp.float32)
    scores = jnp.einsum('brhd,bkhd->bhrk', query_heads, key_heads) * HEAD_DIM ** (-0.5)
    if key_ok is not None:
        scores = jnp.where(key_ok[:, None, None, :], scores, -1e+30)
    highest = lax.optimization_barrier(jnp.max(scores, axis=-1, keepdims=True))
    weights = jnp.exp(scores - highest)
    chances = (weights / lax.optimization_barrier(jnp.sum(weights, axis=-1, keepdims=True))).astype(jnp.bfloat16)
    blended = jnp.einsum('bhrk,bkhd->brhd', chances.astype(jnp.float32), value_heads)
    return blended.astype(jnp.bfloat16).reshape(batch_count * row_count, head_width)

def out_projection(blended, weight):
    group_width = weight.shape[0] // N_MP
    summed = jnp.zeros((blended.shape[0], weight.shape[1]), jnp.float32)
    for member in range(N_MP):
        piece = jnp.dot(blended[:, member * group_width:(member + 1) * group_width], weight[member * group_width:(member + 1) * group_width], preferred_element_type=jnp.float32).astype(jnp.bfloat16)
        piece = lax.optimization_barrier(piece)
        summed = summed + piece.astype(jnp.float32)
    return summed

def gather_blocks(source, listed):
    chosen = source[listed]
    return chosen.reshape(listed.shape[0], listed.shape[1] * BLOCK, source.shape[2])

def reference(grid_in, mesh_in, w_query, w_key, w_value, w_out, norm_gains, enc_list, proc_list, dec_list, grid_count):
    head_width = w_query.shape[2]
    row_ok = jnp.arange(BLOCK)[None, :] < grid_count[:, None]
    mesh_queries = project(normalize(mesh_in, norm_gains[0]), w_query[0]).reshape(-1, BLOCK, head_width)
    grid_normed = normalize(grid_in, norm_gains[1])
    grid_keys = project(grid_normed, w_key[0]).reshape(-1, BLOCK, head_width)
    grid_values = project(grid_normed, w_value[0]).reshape(-1, BLOCK, head_width)
    listed_ok = row_ok[enc_list].reshape(enc_list.shape[0], -1)
    blended = attend(mesh_queries, gather_blocks(grid_keys, enc_list), gather_blocks(grid_values, enc_list), listed_ok)
    mesh = (mesh_in.astype(jnp.float32) + out_projection(blended, w_out[0])).astype(jnp.bfloat16)
    for layer_index in (1, 2):
        normed = normalize(mesh, norm_gains[layer_index + 1])
        queries = project(normed, w_query[layer_index]).reshape(-1, BLOCK, head_width)
        mesh_keys = project(normed, w_key[layer_index]).reshape(-1, BLOCK, head_width)
        mesh_values = project(normed, w_value[layer_index]).reshape(-1, BLOCK, head_width)
        blended = attend(queries, gather_blocks(mesh_keys, proc_list), gather_blocks(mesh_values, proc_list), None)
        mesh = (mesh.astype(jnp.float32) + out_projection(blended, w_out[layer_index])).astype(jnp.bfloat16)
    grid_queries = project(normalize(grid_in, norm_gains[4]), w_query[3]).reshape(-1, BLOCK, head_width)
    mesh_normed = normalize(mesh, norm_gains[5])
    mesh_keys = project(mesh_normed, w_key[3]).reshape(-1, BLOCK, head_width)
    mesh_values = project(mesh_normed, w_value[3]).reshape(-1, BLOCK, head_width)
    blended = attend(grid_queries, gather_blocks(mesh_keys, dec_list), gather_blocks(mesh_values, dec_list), None)
    grid_out = grid_in.astype(jnp.float32) + out_projection(blended, w_out[3])
    grid_out = jnp.where(row_ok.reshape(-1, 1), grid_out, 0.0).astype(jnp.bfloat16)
    return (grid_out, mesh)
```

```python
import functools

import jax
import jax.numpy as jnp
from jax import lax
from jax.experimental import pallas as pl
from jax.experimental.pallas import tpu as pltpu
from jax.sharding import PartitionSpec as P

HEAD_DIM = 64
BLOCK = 128
REACH = 2
SLOTS = 2 * REACH + 1
EPS = 1e-05
NEG = -1e30
F32 = jnp.float32
BF16 = jnp.bfloat16
MESH = pl.DeviceIdType.MESH


def dot_nt(a, b):
    return lax.dot_general(a, b, (((1,), (1,)), ((), ())), preferred_element_type=F32)


def dot_nn(a, b):
    return jnp.dot(a, b, preferred_element_type=F32)


def kernel(
    sizes,
    enc_ref, proc_ref, dec_ref, count_ref,
    grid_ref, mesh_ref, wq_ref, wk_ref, wv_ref, wo_ref, gains_ref,
    gout_ref, mout_ref,
    gfull, mstate, wqkv, wofull, wolast, nbuf, nbuf2,
    qwin, member, kgrid, vtgrid, qdec, opart, stats, orecv, srecv,
    kvwins, oag, oagd,
    lsem, bsem_s, bsem_r, gsem_s, gsem_r, wsem_s, wsem_r, w3sem_s, w3sem_r,
    qsem_s, qsem_r, msem_s, msem_r, osem_s, osem_r, tsem_s, tsem_r,
    kvsem_s, kvsem_r, asem_s, asem_r, dsem_s, dsem_r,
):
    n_nodes, n_mp, chunks = sizes
    node = lax.axis_index("nodes")
    m = lax.axis_index("mp")
    rows_g, feat = grid_ref.shape
    rows_m = mesh_ref.shape[0]
    width = feat * n_mp
    hw = wq_ref.shape[2]
    heads = hw // HEAD_DIM
    gb = rows_g // BLOCK
    mb = rows_m // BLOCK
    chunk = rows_g // chunks
    cb = chunk // BLOCK
    layers = wq_ref.shape[0]
    peer = {1: m + 1 - 2 * (m % 2), 2: (m + 2) % 4, 3: 3 - m}

    def cols(who, size):
        return pl.ds(pl.multiple_of(who * size, size), size)

    def exists(off):
        return jnp.logical_and(node + off >= 0, node + off < n_nodes)

    pending = []

    def send_mp(src, dst, ssem, rsem, r):
        c = pltpu.make_async_remote_copy(
            src_ref=src, dst_ref=dst, send_sem=ssem, recv_sem=rsem,
            device_id={"mp": peer[r]}, device_id_type=MESH)
        c.start()
        pending.append(c)

    def recv_mp(ref, ssem, rsem, r):
        pltpu.make_async_remote_copy(
            src_ref=ref, dst_ref=ref, send_sem=ssem, recv_sem=rsem,
            device_id={"mp": peer[r]}, device_id_type=MESH).wait_recv()

    def node_copy(src, dst, ssem, rsem, off):
        return pltpu.make_async_remote_copy(
            src_ref=src, dst_ref=dst, send_sem=ssem, recv_sem=rsem,
            device_id={"nodes": node + off}, device_id_type=MESH)

    local = {}

    def load(name, src, dst, index):
        c = pltpu.make_async_copy(src, dst, lsem.at[index])
        c.start()
        local[name] = c

    load("mesh", mesh_ref, mstate.at[:, cols(m, feat)], 0)
    load("wq0", wq_ref.at[0], wqkv.at[0, :, 0:hw], 1)
    load("grid", grid_ref, gfull.at[:, cols(m, feat)], 2)
    load("wk", wk_ref, wqkv.at[:, :, hw:2 * hw], 3)
    load("wv", wv_ref, wqkv.at[:, :, 2 * hw:3 * hw], 4)
    load("wq1", wq_ref.at[1:layers], wqkv.at[1:layers, :, 0:hw], 5)
    load("wo", wo_ref.at[0:layers - 1], wofull.at[:, cols(m, hw), :], 6)
    load("wo3", wo_ref.at[layers - 1, :, cols(m, feat)], wolast.at[cols(m, hw), :], 7)

    for slot in range(SLOTS):
        off = slot - REACH
        if off == 0:
            continue

        @pl.when(jnp.logical_not(exists(off)))
        def _(slot=slot):
            orecv[slot] = jnp.zeros(orecv.shape[1:], BF16)
            srecv[slot] = jnp.full(srecv.shape[1:], NEG, F32)
            for l in range(layers - 1):
                kvwins[l][slot * mb:(slot + 1) * mb] = jnp.zeros((mb,) + kvwins[l].shape[1:], BF16)

    barrier = pltpu.get_barrier_semaphore()
    for r in (1, 2, 3):
        pl.semaphore_signal(barrier, inc=1, device_id={"mp": peer[r]}, device_id_type=MESH)
    for off in range(-REACH, REACH + 1):
        if off == 0:
            continue

        @pl.when(exists(off))
        def _(off=off):
            pl.semaphore_signal(barrier, inc=1, device_id={"nodes": node + off}, device_id_type=MESH)
    near = jnp.minimum(node, REACH) + jnp.minimum(n_nodes - 1 - node, REACH)
    pl.semaphore_wait(barrier, 3 + near)

    for r in (2, 1):
        send_mp(mesh_ref, mstate.at[:, cols(m, feat)], bsem_s.at[r - 1], bsem_r.at[r - 1], r)

    def grid_rows(c):
        return pl.ds(c * chunk, chunk)

    for c in range(chunks):
        for r in (2, 1):
            send_mp(grid_ref.at[grid_rows(c), :], gfull.at[grid_rows(c), cols(m, feat)],
                    gsem_s.at[c, r - 1], gsem_r.at[c, r - 1], r)

    def wo_send(l):
        for r in (2, 1):
            send_mp(wo_ref.at[l], wofull.at[l, cols(m, hw), :],
                    wsem_s.at[l, r - 1], wsem_r.at[l, r - 1], r)

    def wo_relay(l):
        part = wofull.at[l, cols(peer[2], hw), :]
        recv_mp(part, wsem_s.at[l, 1], wsem_r.at[l, 1], 2)
        send_mp(part, part, wsem_s.at[l, 2], wsem_r.at[l, 2], 1)

    def wo_finish(l):
        for r in (1, 3):
            recv_mp(wofull.at[l, cols(peer[r], hw), :], wsem_s.at[l, r - 1], wsem_r.at[l, r - 1], r)

    part = mstate.at[:, cols(peer[2], feat)]
    recv_mp(part, bsem_s.at[1], bsem_r.at[1], 2)
    send_mp(part, part, bsem_s.at[2], bsem_r.at[2], 1)
    state_relay = pending.pop()
    for r in (1, 3):
        recv_mp(mstate.at[:, cols(peer[r], feat)], bsem_s.at[r - 1], bsem_r.at[r - 1], r)
    local["mesh"].wait()

    def norm(src, start, count, targets, tile=64):
        def step(i, carry):
            at = pl.multiple_of(i * tile, tile)
            x = src[pl.ds(pl.multiple_of(start + at, tile), tile), :].astype(F32)
            x = x - jnp.mean(x, axis=-1, keepdims=True)
            spread = jnp.mean(x * x, axis=-1, keepdims=True)
            x = x * lax.rsqrt(spread + EPS)
            for dst, g in targets:
                dst[pl.ds(at, tile), :] = (x * gains_ref[g:g + 1, :]).astype(BF16)
            return carry
        lax.fori_loop(0, count // tile, step, 0)

    norm(mstate, 0, rows_m, [(nbuf, 0)])
    local["wq0"].wait()
    qwin[REACH] = (dot_nn(nbuf[0:rows_m, :], wqkv[0, :, 0:hw]).astype(BF16) * BF16(HEAD_DIM ** -0.5)).astype(BF16)

    own_block = lax.broadcasted_iota(jnp.int32, (gb, rows_m), 1) // BLOCK
    block_row = lax.broadcasted_iota(jnp.int32, (gb, rows_m), 0)

    def members(off):
        wanted = (node + off) * gb + block_row
        hit = jnp.zeros((gb, rows_m), jnp.bool_)
        for b in range(mb):
            for j in range(enc_ref.shape[1]):
                hit = hit | ((wanted == enc_ref[b, j]) & (own_block == b))
        return jnp.where(hit, 1.0, 0.0).astype(F32)

    member[REACH] = members(0)

    def q_copies(slot):
        off = slot - REACH
        a = node_copy(qwin.at[REACH], qwin.at[REACH - off], qsem_s.at[slot], qsem_r.at[REACH - off], off)
        b = node_copy(member.at[SLOTS + slot], member.at[REACH - off],
                      msem_s.at[slot], msem_r.at[REACH - off], off)
        return a, b

    remote_slots = [s for s in range(SLOTS) if s != REACH]
    for slot in remote_slots:
        @pl.when(exists(slot - REACH))
        def _(slot=slot):
            member[SLOTS + slot] = members(slot - REACH)
            for c in q_copies(slot):
                c.start()

    local["grid"].wait()
    local["wk"].wait()
    local["wv"].wait()
    local["wq1"].wait()

    def grid_chunk(c):
        norm(gfull, c * chunk, chunk, [(nbuf, 1), (nbuf2, 4)])
        kv = dot_nn(nbuf[0:chunk, :], wqkv[0, :, hw:3 * hw])
        kgrid[grid_rows(c), :] = kv[:, 0:hw].astype(BF16)
        vtgrid[:, c * chunk:(c + 1) * chunk] = kv[:, hw:].T.astype(BF16)
        qd = dot_nn(nbuf2[0:chunk, :], wqkv[layers - 1, :, 0:hw]).astype(BF16)
        qdec[grid_rows(c), :] = (qd * BF16(HEAD_DIM ** -0.5)).astype(BF16)

    for c in range(chunks + 1):
        if c < chunks:
            part = gfull.at[grid_rows(c), cols(peer[2], feat)]
            recv_mp(part, gsem_s.at[c, 1], gsem_r.at[c, 1], 2)
            send_mp(part, part, gsem_s.at[c, 2], gsem_r.at[c, 2], 1)
        if c == 0:
            wo_send(0)
        if c >= 1:
            for r in (1, 3):
                recv_mp(gfull.at[grid_rows(c - 1), cols(peer[r], feat)],
                        gsem_s.at[c - 1, r - 1], gsem_r.at[c - 1, r - 1], r)
            grid_chunk(c - 1)
    wo_relay(0)
    local["wo"].wait()

    lane_head = lax.broadcasted_iota(jnp.int32, (1, hw), 1) // HEAD_DIM
    row_in_block = lax.broadcasted_iota(jnp.int32, (BLOCK, 1), 0)

    def for_head(q, h):
        return jnp.where(lane_head == h, q, jnp.zeros_like(q))

    def o_copies(slot):
        back = slot - REACH
        a = node_copy(opart.at[slot], orecv.at[REACH - back], osem_s.at[slot], osem_r.at[REACH - back], back)
        b = node_copy(stats.at[slot], srecv.at[REACH - back], tsem_s.at[slot], tsem_r.at[REACH - back], back)
        return a, b

    def encode(i, carry):
        slot = i + i // 2 - 4 * (i // 4)
        off = slot - REACH
        remote = i < 2 * REACH

        @pl.when(jnp.logical_and(remote, exists(off)))
        def _():
            node_copy(qwin.at[slot], qwin.at[slot], qsem_s.at[slot], qsem_r.at[slot], off).wait_recv()
            node_copy(member.at[slot], member.at[slot], msem_s.at[slot], msem_r.at[slot], off).wait_recv()

        @pl.when(exists(off))
        def _():
            q = qwin[slot]
            listed = member[slot]
            for h in range(heads):
                qh = for_head(q, h)
                scores = []
                for c in range(gb):
                    ok = (row_in_block < count_ref[node * gb + c]) & (listed[c:c + 1, :] > 0.5)
                    s = dot_nt(kgrid[c * BLOCK:(c + 1) * BLOCK, :], qh)
                    scores.append(jnp.where(ok, s, NEG))
                top = functools.reduce(jnp.maximum, scores)
                top = jnp.max(top, axis=0, keepdims=True)
                probs = [jnp.exp(s - top) for s in scores]
                total = functools.reduce(jnp.add, probs)
                total = jnp.sum(total, axis=0, keepdims=True)
                p = jnp.concatenate([x.astype(BF16) for x in probs], axis=0)
                o = dot_nn(vtgrid[h * HEAD_DIM:(h + 1) * HEAD_DIM, :], p)
                opart[slot, h * HEAD_DIM:(h + 1) * HEAD_DIM, :] = o.astype(BF16)
                stats[slot, h:h + 1, :] = top
                stats[slot, heads + h:heads + h + 1, :] = total

        @pl.when(jnp.logical_and(remote, exists(off)))
        def _():
            for c in o_copies(slot):
                c.start()
        return carry

    lax.fori_loop(0, SLOTS, encode, 0)

    for slot in remote_slots:
        @pl.when(exists(slot - REACH))
        def _(slot=slot):
            off = slot - REACH
            node_copy(orecv.at[slot], orecv.at[slot], osem_s.at[slot], osem_r.at[slot], off).wait_recv()
            node_copy(srecv.at[slot], srecv.at[slot], tsem_s.at[slot], tsem_r.at[slot], off).wait_recv()

    merged = []
    for h in range(heads):
        tops = [stats[REACH, h:h + 1, :] if s == REACH else srecv[s, h:h + 1, :] for s in range(SLOTS)]
        sums = [stats[REACH, heads + h:heads + h + 1, :] if s == REACH else srecv[s, heads + h:heads + h + 1, :]
                for s in range(SLOTS)]
        top = functools.reduce(jnp.maximum, tops)
        total = jnp.zeros_like(top)
        blended = jnp.zeros((HEAD_DIM, rows_m), F32)
        for s in range(SLOTS):
            scale = jnp.exp(tops[s] - top)
            total = total + scale * sums[s]
            src = opart if s == REACH else orecv
            blended = blended + scale * src[s, h * HEAD_DIM:(h + 1) * HEAD_DIM, :].astype(F32)
        merged.append(blended / total)

    def mesh_update(l, merged_t):
        oag[l, :, cols(m, hw)] = merged_t.T.astype(BF16)
        for r in (2, 3, 1):
            src = oag.at[l, :, cols(m, hw)]
            send_mp(src, src, asem_s.at[l, r - 1], asem_r.at[l, r - 1], r)
        if l + 1 < layers - 1:
            wo_send(l + 1)
        else:
            for r in (2, 3, 1):
                send_mp(wo_ref.at[layers - 1, :, cols(peer[r], feat)], wolast.at[cols(m, hw), :],
                        w3sem_s.at[r - 1], w3sem_r.at[r - 1], r)
        wo_finish(l)
        for r in (1, 2, 3):
            recv_mp(oag.at[l, :, cols(peer[r], hw)], asem_s.at[l, r - 1], asem_r.at[l, r - 1], r)
        step = 256
        for j in range(0, width, step):
            update = dot_nn(oag[l], wofull[l, :, j:j + step])
            mstate[:, j:j + step] = (mstate[:, j:j + step].astype(F32) + update).astype(BF16)

    state_relay.wait_send()
    mesh_update(0, jnp.concatenate(merged, axis=0))

    def kv_copy(l, slot):
        off = slot - REACH
        return node_copy(kvwins[l].at[pl.ds(REACH * mb, mb)], kvwins[l].at[pl.ds((REACH - off) * mb, mb)],
                         kvsem_s.at[l, slot], kvsem_r.at[l, REACH - off], off)

    def spread_kv(l, weight_layer):
        kv = dot_nn(nbuf[0:rows_m, :], wqkv[weight_layer, :, hw:3 * hw])
        vt = kv[:, hw:].T
        for b in range(mb):
            kvwins[l][REACH * mb + b, 0] = kv[b * BLOCK:(b + 1) * BLOCK, 0:hw].astype(BF16)
            kvwins[l][REACH * mb + b, 1] = vt[:, b * BLOCK:(b + 1) * BLOCK].astype(BF16)
        for slot in remote_slots:
            @pl.when(exists(slot - REACH))
            def _(slot=slot):
                kv_copy(l, slot).start()

    def collect_kv(l):
        for slot in remote_slots:
            @pl.when(exists(slot - REACH))
            def _(slot=slot):
                part = kvwins[l].at[pl.ds(slot * mb, mb)]
                node_copy(part, part, kvsem_s.at[l, slot], kvsem_r.at[l, slot], slot - REACH).wait_recv()

    def attend(l, q, places):
        keys = jnp.concatenate([kvwins[l][at, 0] for at in places], axis=0)
        values_t = jnp.concatenate([kvwins[l][at, 1] for at in places], axis=1)
        out = []
        for h in range(heads):
            s = dot_nt(keys, for_head(q, h))
            p = jnp.exp(s - jnp.max(s, axis=0, keepdims=True))
            total = jnp.sum(p, axis=0, keepdims=True)
            o = dot_nn(values_t[h * HEAD_DIM:(h + 1) * HEAD_DIM, :], p.astype(BF16))
            out.append(o / total)
        return jnp.concatenate(out, axis=0)

    def place(block):
        return jnp.clip(block - (node - REACH) * mb, 0, SLOTS * mb - 1)

    for l in range(1, layers - 1):
        norm(mstate, 0, rows_m, [(nbuf, l + 1)])
        spread_kv(l - 1, l)
        q = dot_nn(nbuf[0:rows_m, :], wqkv[l, :, 0:hw]).astype(BF16)
        q = (q * BF16(HEAD_DIM ** -0.5)).astype(BF16)
        wo_relay(l)
        collect_kv(l - 1)
        blended = []
        for b in range(mb):
            places = [place(proc_ref[b, j]) for j in range(proc_ref.shape[1])]
            blended.append(attend(l - 1, q[b * BLOCK:(b + 1) * BLOCK, :], places))
        mesh_update(l, jnp.concatenate(blended, axis=1))

    last = layers - 2
    norm(mstate, 0, rows_m, [(nbuf, layers + 1)])
    spread_kv(last, layers - 1)
    mout_ref[...] = mstate[:, cols(m, feat)]
    local["wo3"].wait()
    for r in (1, 2, 3):
        recv_mp(wolast.at[cols(peer[r], hw), :], w3sem_s.at[r - 1], w3sem_r.at[r - 1], r)
    collect_kv(last)
    for c in range(chunks):
        for b in range(c * cb, (c + 1) * cb):
            places = [place(dec_ref[b, j]) for j in range(dec_ref.shape[1])]
            rows = slice(b * BLOCK, (b + 1) * BLOCK)
            oagd[rows, cols(m, hw)] = attend(last, qdec[rows, :], places).T.astype(BF16)
        src = oagd.at[grid_rows(c), cols(m, hw)]
        for r in (2, 1):
            send_mp(src, src, dsem_s.at[c, r - 1], dsem_r.at[c, r - 1], r)
        if c >= 1:
            part = oagd.at[grid_rows(c - 1), cols(peer[2], hw)]
            recv_mp(part, dsem_s.at[c - 1, 1], dsem_r.at[c - 1, 1], 2)
            send_mp(part, part, dsem_s.at[c - 1, 2], dsem_r.at[c - 1, 2], 1)
    for c in range(chunks):
        if c == chunks - 1:
            part = oagd.at[grid_rows(c), cols(peer[2], hw)]
            recv_mp(part, dsem_s.at[c, 1], dsem_r.at[c, 1], 2)
            send_mp(part, part, dsem_s.at[c, 2], dsem_r.at[c, 2], 1)
        for r in (1, 3):
            recv_mp(oagd.at[grid_rows(c), cols(peer[r], hw)], dsem_s.at[c, r - 1], dsem_r.at[c, r - 1], r)
        update = dot_nn(oagd[grid_rows(c), :], wolast[...])
        whole = gfull[grid_rows(c), cols(m, feat)].astype(F32) + update
        for b in range(cb):
            ok = row_in_block < count_ref[node * gb + c * cb + b]
            piece = jnp.where(ok, whole[b * BLOCK:(b + 1) * BLOCK, :], 0.0)
            gout_ref[pl.ds((c * cb + b) * BLOCK, BLOCK), :] = piece.astype(BF16)

    for c in pending:
        c.wait_send()
    for slot in remote_slots:
        @pl.when(exists(slot - REACH))
        def _(slot=slot):
            for c in q_copies(slot) + o_copies(slot):
                c.wait_send()
            for l in range(layers - 1):
                kv_copy(l, slot).wait_send()


def per_device(n_nodes, n_mp, grid_in, mesh_in, w_query, w_key, w_value, w_out, norm_gains,
               enc_list, proc_list, dec_list, grid_count):
    rows_g, feat = grid_in.shape
    rows_m = mesh_in.shape[0]
    width = feat * n_mp
    layers, _, hw = w_query.shape
    heads = hw // HEAD_DIM
    gb, mb = rows_g // BLOCK, rows_m // BLOCK
    chunks = gb // 2 if gb % 2 == 0 else gb
    chunk = rows_g // chunks
    norm_rows = max(chunk, rows_m)
    dma = lambda *shape: pltpu.SemaphoreType.DMA(shape)
    vm = pltpu.VMEM
    scratch = [
        vm((rows_g, width), BF16),
        vm((rows_m, width), BF16),
        vm((layers, width, 3 * hw), BF16),
        vm((layers - 1, hw * n_mp, width), BF16),
        vm((hw * n_mp, feat), BF16),
        vm((norm_rows, width), BF16),
        vm((norm_rows, width), BF16),
        vm((SLOTS, rows_m, hw), BF16),
        vm((2 * SLOTS, gb, rows_m), F32),
        vm((rows_g, hw), BF16),
        vm((hw, rows_g), BF16),
        vm((rows_g, hw), BF16),
        vm((SLOTS, hw, rows_m), BF16),
        vm((SLOTS, max(8, 2 * heads), rows_m), F32),
        vm((SLOTS, hw, rows_m), BF16),
        vm((SLOTS, max(8, 2 * heads), rows_m), F32),
        [vm((SLOTS * mb, 2, BLOCK, hw), BF16) for _ in range(layers - 1)],
        vm((layers - 1, rows_m, hw * n_mp), BF16),
        vm((rows_g, hw * n_mp), BF16),
        dma(8), dma(3), dma(3), dma(chunks, 3), dma(chunks, 3),
        dma(layers - 1, 3), dma(layers - 1, 3), dma(3), dma(3),
        dma(SLOTS), dma(SLOTS), dma(SLOTS), dma(SLOTS), dma(SLOTS), dma(SLOTS), dma(SLOTS), dma(SLOTS),
        dma(layers - 1, SLOTS), dma(layers - 1, SLOTS), dma(layers - 1, 3), dma(layers - 1, 3),
        dma(chunks, 3), dma(chunks, 3),
    ]
    smem = pl.BlockSpec(memory_space=pltpu.SMEM)
    anyspace = pl.BlockSpec(memory_space=pl.ANY)
    vmem = pl.BlockSpec(memory_space=pltpu.VMEM)
    return pl.pallas_call(
        functools.partial(kernel, (n_nodes, n_mp, chunks)),
        out_shape=(
            jax.ShapeDtypeStruct(grid_in.shape, BF16),
            jax.ShapeDtypeStruct(mesh_in.shape, BF16),
        ),
        in_specs=[smem] * 4 + [anyspace] * 6 + [vmem],
        out_specs=(vmem, vmem),
        scratch_shapes=scratch,
        compiler_params=pltpu.CompilerParams(
            collective_id=0, has_side_effects=True, vmem_limit_bytes=60 * 1024 * 1024
        ),
    )(enc_list, proc_list, dec_list, grid_count, grid_in, mesh_in, w_query, w_key, w_value, w_out, norm_gains)


def solution(mesh):
    placed = (
        P("nodes", "mp"),
        P("nodes", "mp"),
        P(None, None, "mp"),
        P(None, None, "mp"),
        P(None, None, "mp"),
        P(None, "mp", None),
        P(),
        P("nodes", None),
        P("nodes", None),
        P("nodes", None),
        P(),
    )
    return jax.shard_map(
        functools.partial(per_device, mesh.shape["nodes"], mesh.shape["mp"]),
        mesh=mesh,
        in_specs=placed,
        out_specs=(P("nodes", "mp"), P("nodes", "mp")),
        check_vma=False,
    )
```

```python
import functools

import jax
import jax.numpy as jnp
from jax import lax
from jax.experimental import pallas as pl
from jax.experimental.pallas import tpu as pltpu
from jax.sharding import PartitionSpec as P

HEAD_DIM = 64
BLOCK = 128
REACH = 2
SLOTS = 2 * REACH + 1
EPS = 1e-05
NEG = -1e30
F32 = jnp.float32
BF16 = jnp.bfloat16
MESH = pl.DeviceIdType.MESH


def dot_nt(a, b):
    return lax.dot_general(a, b, (((1,), (1,)), ((), ())), preferred_element_type=F32)


def dot_nn(a, b):
    return jnp.dot(a, b, preferred_element_type=F32)


def kernel(
    sizes,
    enc_ref, proc_ref, dec_ref, count_ref,
    grid_ref, mesh_ref, wq_ref, wk_ref, wv_ref, wo_ref, gains_ref,
    gout_ref, mout_ref,
    gfull, mstate, wqkv, wofull, wolast, nbuf, nbuf2,
    qwin, member, kgrid, vtgrid, qdec, opart, stats, orecv, srecv,
    kvwins, oag, oagd,
    lsem, bsem_s, bsem_r, gsem_s, gsem_r, wsem_s, wsem_r, w3sem_s, w3sem_r,
    qsem_s, qsem_r, msem_s, msem_r, osem_s, osem_r, tsem_s, tsem_r,
    kvsem_s, kvsem_r, asem_s, asem_r, dsem_s, dsem_r,
):
    n_nodes, n_mp, chunks = sizes
    node = lax.axis_index("nodes")
    m = lax.axis_index("mp")
    rows_g, feat = grid_ref.shape
    rows_m = mesh_ref.shape[0]
    width = feat * n_mp
    hw = wq_ref.shape[2]
    heads = hw // HEAD_DIM
    gb = rows_g // BLOCK
    mb = rows_m // BLOCK
    chunk = rows_g // chunks
    cb = chunk // BLOCK
    layers = wq_ref.shape[0]
    peer = {1: m + 1 - 2 * (m % 2), 2: (m + 2) % 4, 3: 3 - m}

    def cols(who, size):
        return pl.ds(pl.multiple_of(who * size, size), size)

    def exists(off):
        return jnp.logical_and(node + off >= 0, node + off < n_nodes)

    pending = []

    def send_mp(src, dst, ssem, rsem, r):
        c = pltpu.make_async_remote_copy(
            src_ref=src, dst_ref=dst, send_sem=ssem, recv_sem=rsem,
            device_id={"mp": peer[r]}, device_id_type=MESH)
        c.start()
        pending.append(c)

    def recv_mp(ref, ssem, rsem, r):
        pltpu.make_async_remote_copy(
            src_ref=ref, dst_ref=ref, send_sem=ssem, recv_sem=rsem,
            device_id={"mp": peer[r]}, device_id_type=MESH).wait_recv()

    def node_copy(src, dst, ssem, rsem, off):
        return pltpu.make_async_remote_copy(
            src_ref=src, dst_ref=dst, send_sem=ssem, recv_sem=rsem,
            device_id={"nodes": node + off}, device_id_type=MESH)

    local = {}

    def load(name, src, dst, index):
        c = pltpu.make_async_copy(src, dst, lsem.at[index])
        c.start()
        local[name] = c

    load("mesh", mesh_ref, mstate.at[:, cols(m, feat)], 0)
    load("wq0", wq_ref.at[0], wqkv.at[0, :, 0:hw], 1)
    load("grid", grid_ref, gfull.at[:, cols(m, feat)], 2)
    load("wk", wk_ref, wqkv.at[:, :, hw:2 * hw], 3)
    load("wv", wv_ref, wqkv.at[:, :, 2 * hw:3 * hw], 4)
    load("wq1", wq_ref.at[1:layers], wqkv.at[1:layers, :, 0:hw], 5)
    load("wo", wo_ref.at[0:layers - 1], wofull.at[:, cols(m, hw), :], 6)
    load("wo3", wo_ref.at[layers - 1, :, cols(m, feat)], wolast.at[cols(m, hw), :], 7)

    for slot in range(SLOTS):
        off = slot - REACH
        if off == 0:
            continue

        @pl.when(jnp.logical_not(exists(off)))
        def _(slot=slot):
            orecv[slot] = jnp.zeros(orecv.shape[1:], BF16)
            srecv[slot] = jnp.full(srecv.shape[1:], NEG, F32)
            for l in range(layers - 1):
                kvwins[l][slot * mb:(slot + 1) * mb] = jnp.zeros((mb,) + kvwins[l].shape[1:], BF16)

    barrier = pltpu.get_barrier_semaphore()
    for r in (1, 2, 3):
        pl.semaphore_signal(barrier, inc=1, device_id={"mp": peer[r]}, device_id_type=MESH)
    for off in range(-REACH, REACH + 1):
        if off == 0:
            continue

        @pl.when(exists(off))
        def _(off=off):
            pl.semaphore_signal(barrier, inc=1, device_id={"nodes": node + off}, device_id_type=MESH)
    near = jnp.minimum(node, REACH) + jnp.minimum(n_nodes - 1 - node, REACH)
    pl.semaphore_wait(barrier, 3 + near)

    for r in (2, 1):
        send_mp(mesh_ref, mstate.at[:, cols(m, feat)], bsem_s.at[r - 1], bsem_r.at[r - 1], r)

    def grid_rows(c):
        return pl.ds(c * chunk, chunk)

    for c in range(chunks):
        for r in (2, 1):
            send_mp(grid_ref.at[grid_rows(c), :], gfull.at[grid_rows(c), cols(m, feat)],
                    gsem_s.at[c, r - 1], gsem_r.at[c, r - 1], r)

    def wo_send(l):
        for r in (2, 1):
            send_mp(wo_ref.at[l], wofull.at[l, cols(m, hw), :],
                    wsem_s.at[l, r - 1], wsem_r.at[l, r - 1], r)

    def wo_relay(l):
        part = wofull.at[l, cols(peer[2], hw), :]
        recv_mp(part, wsem_s.at[l, 1], wsem_r.at[l, 1], 2)
        send_mp(part, part, wsem_s.at[l, 2], wsem_r.at[l, 2], 1)

    def wo_finish(l):
        for r in (1, 3):
            recv_mp(wofull.at[l, cols(peer[r], hw), :], wsem_s.at[l, r - 1], wsem_r.at[l, r - 1], r)

    part = mstate.at[:, cols(peer[2], feat)]
    recv_mp(part, bsem_s.at[1], bsem_r.at[1], 2)
    send_mp(part, part, bsem_s.at[2], bsem_r.at[2], 1)
    state_relay = pending.pop()
    for r in (1, 3):
        recv_mp(mstate.at[:, cols(peer[r], feat)], bsem_s.at[r - 1], bsem_r.at[r - 1], r)
    local["mesh"].wait()

    def norm(src, start, count, targets, tile=64):
        def step(i, carry):
            at = pl.multiple_of(i * tile, tile)
            x = src[pl.ds(pl.multiple_of(start + at, tile), tile), :].astype(F32)
            x = x - jnp.mean(x, axis=-1, keepdims=True)
            spread = jnp.mean(x * x, axis=-1, keepdims=True)
            x = x * lax.rsqrt(spread + EPS)
            for dst, g in targets:
                dst[pl.ds(at, tile), :] = (x * gains_ref[g:g + 1, :]).astype(BF16)
            return carry
        lax.fori_loop(0, count // tile, step, 0)

    norm(mstate, 0, rows_m, [(nbuf, 0)])
    local["wq0"].wait()
    qwin[REACH] = (dot_nn(nbuf[0:rows_m, :], wqkv[0, :, 0:hw]).astype(BF16) * BF16(HEAD_DIM ** -0.5)).astype(BF16)

    own_block = lax.broadcasted_iota(jnp.int32, (gb, rows_m), 1) // BLOCK
    block_row = lax.broadcasted_iota(jnp.int32, (gb, rows_m), 0)

    def members(off):
        wanted = (node + off) * gb + block_row
        hit = jnp.zeros((gb, rows_m), jnp.bool_)
        for b in range(mb):
            for j in range(enc_ref.shape[1]):
                hit = hit | ((wanted == enc_ref[b, j]) & (own_block == b))
        return jnp.where(hit, 1.0, 0.0).astype(F32)

    member[REACH] = members(0)

    def q_copies(slot):
        off = slot - REACH
        a = node_copy(qwin.at[REACH], qwin.at[REACH - off], qsem_s.at[slot], qsem_r.at[REACH - off], off)
        b = node_copy(member.at[SLOTS + slot], member.at[REACH - off],
                      msem_s.at[slot], msem_r.at[REACH - off], off)
        return a, b

    remote_slots = [s for s in range(SLOTS) if s != REACH]
    for slot in remote_slots:
        @pl.when(exists(slot - REACH))
        def _(slot=slot):
            member[SLOTS + slot] = members(slot - REACH)
            for c in q_copies(slot):
                c.start()

    local["grid"].wait()
    local["wk"].wait()
    local["wv"].wait()
    local["wq1"].wait()

    def grid_chunk(c):
        norm(gfull, c * chunk, chunk, [(nbuf, 1), (nbuf2, 4)])
        kv = dot_nn(nbuf[0:chunk, :], wqkv[0, :, hw:3 * hw])
        kgrid[grid_rows(c), :] = kv[:, 0:hw].astype(BF16)
        vtgrid[:, c * chunk:(c + 1) * chunk] = kv[:, hw:].T.astype(BF16)
        qd = dot_nn(nbuf2[0:chunk, :], wqkv[layers - 1, :, 0:hw]).astype(BF16)
        qdec[grid_rows(c), :] = (qd * BF16(HEAD_DIM ** -0.5)).astype(BF16)

    for c in range(chunks + 1):
        if c < chunks:
            part = gfull.at[grid_rows(c), cols(peer[2], feat)]
            recv_mp(part, gsem_s.at[c, 1], gsem_r.at[c, 1], 2)
            send_mp(part, part, gsem_s.at[c, 2], gsem_r.at[c, 2], 1)
        if c == 0:
            wo_send(0)
        if c >= 1:
            for r in (1, 3):
                recv_mp(gfull.at[grid_rows(c - 1), cols(peer[r], feat)],
                        gsem_s.at[c - 1, r - 1], gsem_r.at[c - 1, r - 1], r)
            grid_chunk(c - 1)
    wo_relay(0)
    local["wo"].wait()

    lane_head = lax.broadcasted_iota(jnp.int32, (1, hw), 1) // HEAD_DIM
    row_in_block = lax.broadcasted_iota(jnp.int32, (BLOCK, 1), 0)

    def for_head(q, h):
        return jnp.where(lane_head == h, q, jnp.zeros_like(q))

    def o_copies(slot):
        back = slot - REACH
        a = node_copy(opart.at[slot], orecv.at[REACH - back], osem_s.at[slot], osem_r.at[REACH - back], back)
        b = node_copy(stats.at[slot], srecv.at[REACH - back], tsem_s.at[slot], tsem_r.at[REACH - back], back)
        return a, b

    def encode(i, carry):
        slot = i + i // 2 - 4 * (i // 4)
        off = slot - REACH
        remote = i < 2 * REACH

        @pl.when(jnp.logical_and(remote, exists(off)))
        def _():
            node_copy(qwin.at[slot], qwin.at[slot], qsem_s.at[slot], qsem_r.at[slot], off).wait_recv()
            node_copy(member.at[slot], member.at[slot], msem_s.at[slot], msem_r.at[slot], off).wait_recv()

        @pl.when(exists(off))
        def _():
            q = qwin[slot]
            listed = member[slot]
            for h in range(heads):
                qh = for_head(q, h)
                scores = []
                for c in range(gb):
                    ok = (row_in_block < count_ref[node * gb + c]) & (listed[c:c + 1, :] > 0.5)
                    s = dot_nt(kgrid[c * BLOCK:(c + 1) * BLOCK, :], qh)
                    scores.append(jnp.where(ok, s, NEG))
                top = functools.reduce(jnp.maximum, scores)
                top = jnp.max(top, axis=0, keepdims=True)
                probs = [jnp.exp(s - top) for s in scores]
                total = functools.reduce(jnp.add, probs)
                total = jnp.sum(total, axis=0, keepdims=True)
                p = jnp.concatenate([x.astype(BF16) for x in probs], axis=0)
                o = dot_nn(vtgrid[h * HEAD_DIM:(h + 1) * HEAD_DIM, :], p)
                opart[slot, h * HEAD_DIM:(h + 1) * HEAD_DIM, :] = o.astype(BF16)
                stats[slot, h:h + 1, :] = top
                stats[slot, heads + h:heads + h + 1, :] = total

        @pl.when(jnp.logical_and(remote, exists(off)))
        def _():
            for c in o_copies(slot):
                c.start()
        return carry

    lax.fori_loop(0, SLOTS, encode, 0)

    for slot in remote_slots:
        @pl.when(exists(slot - REACH))
        def _(slot=slot):
            off = slot - REACH
            node_copy(orecv.at[slot], orecv.at[slot], osem_s.at[slot], osem_r.at[slot], off).wait_recv()
            node_copy(srecv.at[slot], srecv.at[slot], tsem_s.at[slot], tsem_r.at[slot], off).wait_recv()

    def merge(b):
        lanes = slice(b * BLOCK, (b + 1) * BLOCK)
        merged = []
        for h in range(heads):
            rows = slice(h * HEAD_DIM, (h + 1) * HEAD_DIM)
            tops, sums, parts = [], [], []
            for s in range(SLOTS):
                st, part = (stats, opart) if s == REACH else (srecv, orecv)
                tops.append(st[s, h:h + 1, lanes])
                sums.append(st[s, heads + h:heads + h + 1, lanes])
                parts.append(part[s, rows, lanes].astype(F32))
            top = functools.reduce(jnp.maximum, tops)
            scales = [jnp.exp(t - top) for t in tops]
            total = functools.reduce(jnp.add, [a * x for a, x in zip(scales, sums)])
            blended = functools.reduce(jnp.add, [a * x for a, x in zip(scales, parts)])
            merged.append(blended / total)
        return jnp.concatenate(merged, axis=0)

    def block_rows(b):
        return pl.ds(b * BLOCK, BLOCK)

    def share(l, b, blended_t):
        src = oag.at[l, block_rows(b), cols(m, hw)]
        oag[l, block_rows(b), cols(m, hw)] = blended_t.T.astype(BF16)
        for r in (2, 3, 1):
            send_mp(src, src, asem_s.at[l, b, r - 1], asem_r.at[l, b, r - 1], r)

    def kv_copy(l, slot, b):
        off = slot - REACH
        return node_copy(kvwins[l].at[REACH * mb + b], kvwins[l].at[(REACH - off) * mb + b],
                         kvsem_s.at[l, slot, b], kvsem_r.at[l, REACH - off, b], off)

    def update(l, b):
        for r in (1, 2, 3):
            recv_mp(oag.at[l, block_rows(b), cols(peer[r], hw)],
                    asem_s.at[l, b, r - 1], asem_r.at[l, b, r - 1], r)
        step = 256
        for j in range(0, width, step):
            change = dot_nn(oag[l, block_rows(b), :], wofull[l, :, j:j + step])
            mstate[block_rows(b), j:j + step] = (mstate[block_rows(b), j:j + step].astype(F32) + change).astype(BF16)
        norm(mstate, b * BLOCK, BLOCK, [(nbuf.at[block_rows(b), :], l + 2 if l + 2 < layers else layers + 1)])
        kv = dot_nn(nbuf[block_rows(b), :], wqkv[l + 1, :, hw:3 * hw])
        kvwins[l][REACH * mb + b, 0] = kv[:, 0:hw].astype(BF16)
        kvwins[l][REACH * mb + b, 1] = kv[:, hw:].T.astype(BF16)
        for slot in remote_slots:
            @pl.when(exists(slot - REACH))
            def _(slot=slot):
                kv_copy(l, slot, b).start()

    def collect_kv(l):
        for slot in remote_slots:
            @pl.when(exists(slot - REACH))
            def _(slot=slot):
                for b in range(mb):
                    part = kvwins[l].at[slot * mb + b]
                    node_copy(part, part, kvsem_s.at[l, slot, b], kvsem_r.at[l, slot, b],
                              slot - REACH).wait_recv()

    def attend(l, q, places):
        keys = jnp.concatenate([kvwins[l][at, 0] for at in places], axis=0)
        values_t = jnp.concatenate([kvwins[l][at, 1] for at in places], axis=1)
        out = []
        for h in range(heads):
            s = dot_nt(keys, for_head(q, h))
            p = jnp.exp(s - jnp.max(s, axis=0, keepdims=True))
            total = jnp.sum(p, axis=0, keepdims=True)
            o = dot_nn(values_t[h * HEAD_DIM:(h + 1) * HEAD_DIM, :], p.astype(BF16))
            out.append(o / total)
        return jnp.concatenate(out, axis=0)

    def place(block):
        return jnp.clip(block - (node - REACH) * mb, 0, SLOTS * mb - 1)

    state_relay.wait_send()
    for l in range(layers - 1):
        if l > 0:
            q = dot_nn(nbuf[0:rows_m, :], wqkv[l, :, 0:hw]).astype(BF16)
            q = (q * BF16(HEAD_DIM ** -0.5)).astype(BF16)
            wo_relay(l)
            collect_kv(l - 1)
        for b in range(mb):
            if l == 0:
                blended_t = merge(b)
            else:
                places = [place(proc_ref[b, j]) for j in range(proc_ref.shape[1])]
                blended_t = attend(l - 1, q[b * BLOCK:(b + 1) * BLOCK, :], places)
            share(l, b, blended_t)
        if l + 1 < layers - 1:
            wo_send(l + 1)
        else:
            for r in (2, 3, 1):
                send_mp(wo_ref.at[layers - 1, :, cols(peer[r], feat)], wolast.at[cols(m, hw), :],
                        w3sem_s.at[r - 1], w3sem_r.at[r - 1], r)
        wo_finish(l)
        for b in range(mb):
            update(l, b)

    last = layers - 2
    mout_ref[...] = mstate[:, cols(m, feat)]
    local["wo3"].wait()
    for r in (1, 2, 3):
        recv_mp(wolast.at[cols(peer[r], hw), :], w3sem_s.at[r - 1], w3sem_r.at[r - 1], r)
    collect_kv(last)
    for c in range(chunks):
        for b in range(c * cb, (c + 1) * cb):
            places = [place(dec_ref[b, j]) for j in range(dec_ref.shape[1])]
            rows = slice(b * BLOCK, (b + 1) * BLOCK)
            oagd[rows, cols(m, hw)] = attend(last, qdec[rows, :], places).T.astype(BF16)
        src = oagd.at[grid_rows(c), cols(m, hw)]
        for r in (2, 1):
            send_mp(src, src, dsem_s.at[c, r - 1], dsem_r.at[c, r - 1], r)
        if c >= 1:
            part = oagd.at[grid_rows(c - 1), cols(peer[2], hw)]
            recv_mp(part, dsem_s.at[c - 1, 1], dsem_r.at[c - 1, 1], 2)
            send_mp(part, part, dsem_s.at[c - 1, 2], dsem_r.at[c - 1, 2], 1)
    for c in range(chunks):
        if c == chunks - 1:
            part = oagd.at[grid_rows(c), cols(peer[2], hw)]
            recv_mp(part, dsem_s.at[c, 1], dsem_r.at[c, 1], 2)
            send_mp(part, part, dsem_s.at[c, 2], dsem_r.at[c, 2], 1)
        for r in (1, 3):
            recv_mp(oagd.at[grid_rows(c), cols(peer[r], hw)], dsem_s.at[c, r - 1], dsem_r.at[c, r - 1], r)
        change = dot_nn(oagd[grid_rows(c), :], wolast[...])
        whole = gfull[grid_rows(c), cols(m, feat)].astype(F32) + change
        for b in range(cb):
            ok = row_in_block < count_ref[node * gb + c * cb + b]
            piece = jnp.where(ok, whole[b * BLOCK:(b + 1) * BLOCK, :], 0.0)
            gout_ref[pl.ds((c * cb + b) * BLOCK, BLOCK), :] = piece.astype(BF16)

    for c in pending:
        c.wait_send()
    for slot in remote_slots:
        @pl.when(exists(slot - REACH))
        def _(slot=slot):
            for c in q_copies(slot) + o_copies(slot):
                c.wait_send()
            for l in range(layers - 1):
                for b in range(mb):
                    kv_copy(l, slot, b).wait_send()


def per_device(n_nodes, n_mp, grid_in, mesh_in, w_query, w_key, w_value, w_out, norm_gains,
               enc_list, proc_list, dec_list, grid_count):
    rows_g, feat = grid_in.shape
    rows_m = mesh_in.shape[0]
    width = feat * n_mp
    layers, _, hw = w_query.shape
    heads = hw // HEAD_DIM
    gb, mb = rows_g // BLOCK, rows_m // BLOCK
    chunks = gb // 2 if gb % 2 == 0 else gb
    chunk = rows_g // chunks
    norm_rows = max(chunk, rows_m)
    dma = lambda *shape: pltpu.SemaphoreType.DMA(shape)
    vm = pltpu.VMEM
    scratch = [
        vm((rows_g, width), BF16),
        vm((rows_m, width), BF16),
        vm((layers, width, 3 * hw), BF16),
        vm((layers - 1, hw * n_mp, width), BF16),
        vm((hw * n_mp, feat), BF16),
        vm((norm_rows, width), BF16),
        vm((norm_rows, width), BF16),
        vm((SLOTS, rows_m, hw), BF16),
        vm((2 * SLOTS, gb, rows_m), F32),
        vm((rows_g, hw), BF16),
        vm((hw, rows_g), BF16),
        vm((rows_g, hw), BF16),
        vm((SLOTS, hw, rows_m), BF16),
        vm((SLOTS, max(8, 2 * heads), rows_m), F32),
        vm((SLOTS, hw, rows_m), BF16),
        vm((SLOTS, max(8, 2 * heads), rows_m), F32),
        [vm((SLOTS * mb, 2, BLOCK, hw), BF16) for _ in range(layers - 1)],
        vm((layers - 1, rows_m, hw * n_mp), BF16),
        vm((rows_g, hw * n_mp), BF16),
        dma(8), dma(3), dma(3), dma(chunks, 3), dma(chunks, 3),
        dma(layers - 1, 3), dma(layers - 1, 3), dma(3), dma(3),
        dma(SLOTS), dma(SLOTS), dma(SLOTS), dma(SLOTS), dma(SLOTS), dma(SLOTS), dma(SLOTS), dma(SLOTS),
        dma(layers - 1, SLOTS, mb), dma(layers - 1, SLOTS, mb), dma(layers - 1, mb, 3), dma(layers - 1, mb, 3),
        dma(chunks, 3), dma(chunks, 3),
    ]
    smem = pl.BlockSpec(memory_space=pltpu.SMEM)
    anyspace = pl.BlockSpec(memory_space=pl.ANY)
    vmem = pl.BlockSpec(memory_space=pltpu.VMEM)
    return pl.pallas_call(
        functools.partial(kernel, (n_nodes, n_mp, chunks)),
        out_shape=(
            jax.ShapeDtypeStruct(grid_in.shape, BF16),
            jax.ShapeDtypeStruct(mesh_in.shape, BF16),
        ),
        in_specs=[smem] * 4 + [anyspace] * 6 + [vmem],
        out_specs=(vmem, vmem),
        scratch_shapes=scratch,
        compiler_params=pltpu.CompilerParams(
            collective_id=0, has_side_effects=True, vmem_limit_bytes=60 * 1024 * 1024
        ),
    )(enc_list, proc_list, dec_list, grid_count, grid_in, mesh_in, w_query, w_key, w_value, w_out, norm_gains)


def solution(mesh):
    placed = (
        P("nodes", "mp"),
        P("nodes", "mp"),
        P(None, None, "mp"),
        P(None, None, "mp"),
        P(None, None, "mp"),
        P(None, "mp", None),
        P(),
        P("nodes", None),
        P("nodes", None),
        P("nodes", None),
        P(),
    )
    return jax.shard_map(
        functools.partial(per_device, mesh.shape["nodes"], mesh.shape["mp"]),
        mesh=mesh,
        in_specs=placed,
        out_specs=(P("nodes", "mp"), P("nodes", "mp")),
        check_vma=False,
    )
```

```python
import functools

import jax
import jax.numpy as jnp
from jax import lax
from jax.experimental import pallas as pl
from jax.experimental.pallas import tpu as pltpu
from jax.sharding import PartitionSpec as P

HEAD_DIM = 64
BLOCK = 128
REACH = 2
SLOTS = 2 * REACH + 1
EPS = 1e-05
NEG = -1e30
F32 = jnp.float32
BF16 = jnp.bfloat16
MESH = pl.DeviceIdType.MESH


def dot_nt(a, b):
    return lax.dot_general(a, b, (((1,), (1,)), ((), ())), preferred_element_type=F32)


def dot_nn(a, b):
    return jnp.dot(a, b, preferred_element_type=F32)


def kernel(
    sizes,
    enc_ref, proc_ref, dec_ref, count_ref,
    grid_ref, mesh_ref, wq_ref, wk_ref, wv_ref, wo_ref, gains_ref,
    gout_ref, mout_ref,
    gfull, mstate, wqkv, wofull, wolast, nbuf, nbuf2,
    qwin, member, kgrid, vtgrid, qdec, opart, oearly, stats, orecv, srecv,
    kvwins, oag, oagd,
    lsem, bsem_s, bsem_r, gsem_s, gsem_r, wsem_s, wsem_r, w3sem_s, w3sem_r,
    qsem_s, qsem_r, msem_s, msem_r, osem_s, osem_r, tsem_s, tsem_r,
    kvsem_s, kvsem_r, asem_s, asem_r, dsem_s, dsem_r,
):
    n_nodes, n_mp, chunks = sizes
    node = lax.axis_index("nodes")
    m = lax.axis_index("mp")
    rows_g, feat = grid_ref.shape
    rows_m = mesh_ref.shape[0]
    width = feat * n_mp
    hw = wq_ref.shape[2]
    heads = hw // HEAD_DIM
    gb = rows_g // BLOCK
    mb = rows_m // BLOCK
    chunk = rows_g // chunks
    cb = chunk // BLOCK
    layers = wq_ref.shape[0]
    peer = {1: m + 1 - 2 * (m % 2), 2: (m + 2) % 4, 3: 3 - m}

    def cols(who, size):
        return pl.ds(pl.multiple_of(who * size, size), size)

    def exists(off):
        return jnp.logical_and(node + off >= 0, node + off < n_nodes)

    pending = []

    def send_mp(src, dst, ssem, rsem, r):
        c = pltpu.make_async_remote_copy(
            src_ref=src, dst_ref=dst, send_sem=ssem, recv_sem=rsem,
            device_id={"mp": peer[r]}, device_id_type=MESH)
        c.start()
        pending.append(c)

    def recv_mp(ref, ssem, rsem, r):
        pltpu.make_async_remote_copy(
            src_ref=ref, dst_ref=ref, send_sem=ssem, recv_sem=rsem,
            device_id={"mp": peer[r]}, device_id_type=MESH).wait_recv()

    def node_copy(src, dst, ssem, rsem, off):
        return pltpu.make_async_remote_copy(
            src_ref=src, dst_ref=dst, send_sem=ssem, recv_sem=rsem,
            device_id={"nodes": node + off}, device_id_type=MESH)

    local = {}

    def load(name, src, dst, index):
        c = pltpu.make_async_copy(src, dst, lsem.at[index])
        c.start()
        local[name] = c

    load("mesh", mesh_ref, mstate.at[:, cols(m, feat)], 0)
    load("wq0", wq_ref.at[0], wqkv.at[0, :, 0:hw], 1)
    load("grid", grid_ref, gfull.at[:, cols(m, feat)], 2)
    load("wk", wk_ref, wqkv.at[:, :, hw:2 * hw], 3)
    load("wv", wv_ref, wqkv.at[:, :, 2 * hw:3 * hw], 4)
    load("wq1", wq_ref.at[1:layers], wqkv.at[1:layers, :, 0:hw], 5)
    load("wo", wo_ref.at[0:layers - 1], wofull.at[:, cols(m, hw), :], 6)
    load("wo3", wo_ref.at[layers - 1, :, cols(m, feat)], wolast.at[cols(m, hw), :], 7)

    for slot in range(SLOTS):
        off = slot - REACH
        if off == 0:
            continue

        @pl.when(jnp.logical_not(exists(off)))
        def _(slot=slot):
            orecv[slot] = jnp.zeros(orecv.shape[1:], BF16)
            srecv[slot] = jnp.full(srecv.shape[1:], NEG, F32)
            for l in range(layers - 1):
                kvwins[l][slot * mb:(slot + 1) * mb] = jnp.zeros((mb,) + kvwins[l].shape[1:], BF16)

    barrier = pltpu.get_barrier_semaphore()
    for r in (1, 2, 3):
        pl.semaphore_signal(barrier, inc=1, device_id={"mp": peer[r]}, device_id_type=MESH)
    for off in range(-REACH, REACH + 1):
        if off == 0:
            continue

        @pl.when(exists(off))
        def _(off=off):
            pl.semaphore_signal(barrier, inc=1, device_id={"nodes": node + off}, device_id_type=MESH)
    near = jnp.minimum(node, REACH) + jnp.minimum(n_nodes - 1 - node, REACH)
    pl.semaphore_wait(barrier, 3 + near)

    for r in (2, 1):
        send_mp(mesh_ref, mstate.at[:, cols(m, feat)], bsem_s.at[r - 1], bsem_r.at[r - 1], r)

    def grid_rows(c):
        return pl.ds(c * chunk, chunk)

    for c in range(chunks):
        for r in (2, 1):
            send_mp(grid_ref.at[grid_rows(c), :], gfull.at[grid_rows(c), cols(m, feat)],
                    gsem_s.at[c, r - 1], gsem_r.at[c, r - 1], r)

    def wo_send(l):
        for r in (2, 1):
            send_mp(wo_ref.at[l], wofull.at[l, cols(m, hw), :],
                    wsem_s.at[l, r - 1], wsem_r.at[l, r - 1], r)

    def wo_relay(l):
        part = wofull.at[l, cols(peer[2], hw), :]
        recv_mp(part, wsem_s.at[l, 1], wsem_r.at[l, 1], 2)
        send_mp(part, part, wsem_s.at[l, 2], wsem_r.at[l, 2], 1)

    def wo_finish(l):
        for r in (1, 3):
            recv_mp(wofull.at[l, cols(peer[r], hw), :], wsem_s.at[l, r - 1], wsem_r.at[l, r - 1], r)

    part = mstate.at[:, cols(peer[2], feat)]
    recv_mp(part, bsem_s.at[1], bsem_r.at[1], 2)
    send_mp(part, part, bsem_s.at[2], bsem_r.at[2], 1)
    state_relay = pending.pop()
    for r in (1, 3):
        recv_mp(mstate.at[:, cols(peer[r], feat)], bsem_s.at[r - 1], bsem_r.at[r - 1], r)
    local["mesh"].wait()

    def norm(src, start, count, targets, tile=64):
        def step(i, carry):
            at = pl.multiple_of(i * tile, tile)
            x = src[pl.ds(pl.multiple_of(start + at, tile), tile), :].astype(F32)
            x = x - jnp.mean(x, axis=-1, keepdims=True)
            spread = jnp.mean(x * x, axis=-1, keepdims=True)
            x = x * lax.rsqrt(spread + EPS)
            for dst, g in targets:
                dst[pl.ds(at, tile), :] = (x * gains_ref[g:g + 1, :]).astype(BF16)
            return carry
        lax.fori_loop(0, count // tile, step, 0)

    norm(mstate, 0, rows_m, [(nbuf, 0)])
    local["wq0"].wait()
    qwin[REACH] = (dot_nn(nbuf[0:rows_m, :], wqkv[0, :, 0:hw]).astype(BF16) * BF16(HEAD_DIM ** -0.5)).astype(BF16)

    own_block = lax.broadcasted_iota(jnp.int32, (gb, rows_m), 1) // BLOCK
    block_row = lax.broadcasted_iota(jnp.int32, (gb, rows_m), 0)

    def members(off):
        wanted = (node + off) * gb + block_row
        hit = jnp.zeros((gb, rows_m), jnp.bool_)
        for b in range(mb):
            for j in range(enc_ref.shape[1]):
                hit = hit | ((wanted == enc_ref[b, j]) & (own_block == b))
        return jnp.where(hit, 1.0, 0.0).astype(F32)

    member[REACH] = members(0)

    def q_copies(slot):
        off = slot - REACH
        a = node_copy(qwin.at[REACH], qwin.at[REACH - off], qsem_s.at[slot], qsem_r.at[REACH - off], off)
        b = node_copy(member.at[SLOTS + slot], member.at[REACH - off],
                      msem_s.at[slot], msem_r.at[REACH - off], off)
        return a, b

    remote_slots = [s for s in range(SLOTS) if s != REACH]
    for slot in remote_slots:
        @pl.when(exists(slot - REACH))
        def _(slot=slot):
            member[SLOTS + slot] = members(slot - REACH)
            for c in q_copies(slot):
                c.start()

    local["grid"].wait()
    local["wk"].wait()
    local["wv"].wait()
    local["wq1"].wait()

    def grid_chunk(c):
        norm(gfull, c * chunk, chunk, [(nbuf, 1), (nbuf2, 4)])
        kv = dot_nn(nbuf[0:chunk, :], wqkv[0, :, hw:3 * hw])
        kgrid[grid_rows(c), :] = kv[:, 0:hw].astype(BF16)
        vtgrid[:, c * chunk:(c + 1) * chunk] = kv[:, hw:].T.astype(BF16)
        qd = dot_nn(nbuf2[0:chunk, :], wqkv[layers - 1, :, 0:hw]).astype(BF16)
        qdec[grid_rows(c), :] = (qd * BF16(HEAD_DIM ** -0.5)).astype(BF16)

    lane_head = lax.broadcasted_iota(jnp.int32, (1, hw), 1) // HEAD_DIM
    row_in_block = lax.broadcasted_iota(jnp.int32, (BLOCK, 1), 0)

    def for_head(q, h):
        return jnp.where(lane_head == h, q, jnp.zeros_like(q))

    def o_copies(slot):
        back = slot - REACH
        a = node_copy(opart.at[slot], orecv.at[REACH - back], osem_s.at[slot], osem_r.at[REACH - back], back)
        b = node_copy(stats.at[slot], srecv.at[REACH - back], tsem_s.at[slot], tsem_r.at[REACH - back], back)
        return a, b

    half = gb // 2

    def encode(late, i, carry):
        slot = i + i // 2 - 4 * (i // 4)
        off = slot - REACH
        remote = i < 2 * REACH

        @pl.when(jnp.logical_and(remote, exists(off)) if not late else False)
        def _():
            node_copy(qwin.at[slot], qwin.at[slot], qsem_s.at[slot], qsem_r.at[slot], off).wait_recv()
            node_copy(member.at[slot], member.at[slot], msem_s.at[slot], msem_r.at[slot], off).wait_recv()

        @pl.when(exists(off))
        def _():
            q = qwin[slot]
            listed = member[slot]
            for h in range(heads):
                qh = for_head(q, h)
                scores = []
                blocks = range(half, gb) if late else range(half)
                for c in blocks:
                    ok = (row_in_block < count_ref[node * gb + c]) & (listed[c:c + 1, :] > 0.5)
                    s = dot_nt(kgrid[c * BLOCK:(c + 1) * BLOCK, :], qh)
                    scores.append(jnp.where(ok, s, NEG))
                top = functools.reduce(jnp.maximum, scores)
                top = jnp.max(top, axis=0, keepdims=True)
                if late:
                    before = stats[slot, h:h + 1, :]
                    top = jnp.maximum(top, before)
                probs = [jnp.exp(s - top) for s in scores]
                total = functools.reduce(jnp.add, probs)
                total = jnp.sum(total, axis=0, keepdims=True)
                p = jnp.concatenate([x.astype(BF16) for x in probs], axis=0)
                keys = slice(blocks[0] * BLOCK, (blocks[-1] + 1) * BLOCK)
                o = dot_nn(vtgrid[h * HEAD_DIM:(h + 1) * HEAD_DIM, keys], p)
                if late:
                    scale = jnp.exp(before - top)
                    total = total + scale * stats[slot, heads + h:heads + h + 1, :]
                    o = o + scale * oearly[slot, h * HEAD_DIM:(h + 1) * HEAD_DIM, :]
                    opart[slot, h * HEAD_DIM:(h + 1) * HEAD_DIM, :] = o.astype(BF16)
                else:
                    oearly[slot, h * HEAD_DIM:(h + 1) * HEAD_DIM, :] = o
                stats[slot, h:h + 1, :] = top
                stats[slot, heads + h:heads + h + 1, :] = total

        @pl.when(jnp.logical_and(remote, exists(off)) if late else False)
        def _():
            for c in o_copies(slot):
                c.start()
        return carry

    for c in range(chunks + 1):
        if c < chunks:
            part = gfull.at[grid_rows(c), cols(peer[2], feat)]
            recv_mp(part, gsem_s.at[c, 1], gsem_r.at[c, 1], 2)
            send_mp(part, part, gsem_s.at[c, 2], gsem_r.at[c, 2], 1)
        if c == 0:
            wo_send(0)
        if c >= 1:
            for r in (1, 3):
                recv_mp(gfull.at[grid_rows(c - 1), cols(peer[r], feat)],
                        gsem_s.at[c - 1, r - 1], gsem_r.at[c - 1, r - 1], r)
            grid_chunk(c - 1)
            if c == half // cb:
                lax.fori_loop(0, SLOTS, functools.partial(encode, False), 0)
    lax.fori_loop(0, SLOTS, functools.partial(encode, True), 0)
    wo_relay(0)
    local["wo"].wait()

    for slot in remote_slots:
        @pl.when(exists(slot - REACH))
        def _(slot=slot):
            off = slot - REACH
            node_copy(orecv.at[slot], orecv.at[slot], osem_s.at[slot], osem_r.at[slot], off).wait_recv()
            node_copy(srecv.at[slot], srecv.at[slot], tsem_s.at[slot], tsem_r.at[slot], off).wait_recv()

    def merge(b):
        lanes = slice(b * BLOCK, (b + 1) * BLOCK)
        merged = []
        for h in range(heads):
            rows = slice(h * HEAD_DIM, (h + 1) * HEAD_DIM)
            tops, sums, parts = [], [], []
            for s in range(SLOTS):
                st, part = (stats, opart) if s == REACH else (srecv, orecv)
                tops.append(st[s, h:h + 1, lanes])
                sums.append(st[s, heads + h:heads + h + 1, lanes])
                parts.append(part[s, rows, lanes].astype(F32))
            top = functools.reduce(jnp.maximum, tops)
            scales = [jnp.exp(t - top) for t in tops]
            total = functools.reduce(jnp.add, [a * x for a, x in zip(scales, sums)])
            blended = functools.reduce(jnp.add, [a * x for a, x in zip(scales, parts)])
            merged.append(blended / total)
        return jnp.concatenate(merged, axis=0)

    def block_rows(b):
        return pl.ds(b * BLOCK, BLOCK)

    def share(l, b, blended_t):
        src = oag.at[l, block_rows(b), cols(m, hw)]
        oag[l, block_rows(b), cols(m, hw)] = blended_t.T.astype(BF16)
        for r in (2, 3, 1):
            send_mp(src, src, asem_s.at[l, b, r - 1], asem_r.at[l, b, r - 1], r)

    def kv_copy(l, slot, b):
        off = slot - REACH
        return node_copy(kvwins[l].at[REACH * mb + b], kvwins[l].at[(REACH - off) * mb + b],
                         kvsem_s.at[l, slot, b], kvsem_r.at[l, REACH - off, b], off)

    def update(l, b):
        for r in (1, 2, 3):
            recv_mp(oag.at[l, block_rows(b), cols(peer[r], hw)],
                    asem_s.at[l, b, r - 1], asem_r.at[l, b, r - 1], r)
        step = 256
        for j in range(0, width, step):
            change = dot_nn(oag[l, block_rows(b), :], wofull[l, :, j:j + step])
            mstate[block_rows(b), j:j + step] = (mstate[block_rows(b), j:j + step].astype(F32) + change).astype(BF16)
        norm(mstate, b * BLOCK, BLOCK, [(nbuf.at[block_rows(b), :], l + 2 if l + 2 < layers else layers + 1)])
        kv = dot_nn(nbuf[block_rows(b), :], wqkv[l + 1, :, hw:3 * hw])
        kvwins[l][REACH * mb + b, 0] = kv[:, 0:hw].astype(BF16)
        kvwins[l][REACH * mb + b, 1] = kv[:, hw:].T.astype(BF16)
        for slot in remote_slots:
            @pl.when(exists(slot - REACH))
            def _(slot=slot):
                kv_copy(l, slot, b).start()

    def collect_kv(l):
        for slot in remote_slots:
            @pl.when(exists(slot - REACH))
            def _(slot=slot):
                for b in range(mb):
                    part = kvwins[l].at[slot * mb + b]
                    node_copy(part, part, kvsem_s.at[l, slot, b], kvsem_r.at[l, slot, b],
                              slot - REACH).wait_recv()

    def attend(l, q, places):
        keys = jnp.concatenate([kvwins[l][at, 0] for at in places], axis=0)
        values_t = jnp.concatenate([kvwins[l][at, 1] for at in places], axis=1)
        out = []
        for h in range(heads):
            s = dot_nt(keys, for_head(q, h))
            p = jnp.exp(s - jnp.max(s, axis=0, keepdims=True))
            total = jnp.sum(p, axis=0, keepdims=True)
            o = dot_nn(values_t[h * HEAD_DIM:(h + 1) * HEAD_DIM, :], p.astype(BF16))
            out.append(o / total)
        return jnp.concatenate(out, axis=0)

    def place(block):
        return jnp.clip(block - (node - REACH) * mb, 0, SLOTS * mb - 1)

    state_relay.wait_send()
    for l in range(layers - 1):
        if l > 0:
            q = dot_nn(nbuf[0:rows_m, :], wqkv[l, :, 0:hw]).astype(BF16)
            q = (q * BF16(HEAD_DIM ** -0.5)).astype(BF16)
            wo_relay(l)
            collect_kv(l - 1)
        for b in range(mb):
            if l == 0:
                blended_t = merge(b)
            else:
                places = [place(proc_ref[b, j]) for j in range(proc_ref.shape[1])]
                blended_t = attend(l - 1, q[b * BLOCK:(b + 1) * BLOCK, :], places)
            share(l, b, blended_t)
        if l + 1 < layers - 1:
            wo_send(l + 1)
        else:
            for r in (2, 3, 1):
                send_mp(wo_ref.at[layers - 1, :, cols(peer[r], feat)], wolast.at[cols(m, hw), :],
                        w3sem_s.at[r - 1], w3sem_r.at[r - 1], r)
        wo_finish(l)
        for b in range(mb):
            update(l, b)

    last = layers - 2
    mout_ref[...] = mstate[:, cols(m, feat)]
    local["wo3"].wait()
    for r in (1, 2, 3):
        recv_mp(wolast.at[cols(peer[r], hw), :], w3sem_s.at[r - 1], w3sem_r.at[r - 1], r)
    collect_kv(last)
    for c in range(chunks):
        for b in range(c * cb, (c + 1) * cb):
            places = [place(dec_ref[b, j]) for j in range(dec_ref.shape[1])]
            rows = slice(b * BLOCK, (b + 1) * BLOCK)
            oagd[rows, cols(m, hw)] = attend(last, qdec[rows, :], places).T.astype(BF16)
        src = oagd.at[grid_rows(c), cols(m, hw)]
        for r in (2, 1):
            send_mp(src, src, dsem_s.at[c, r - 1], dsem_r.at[c, r - 1], r)
        if c >= 1:
            part = oagd.at[grid_rows(c - 1), cols(peer[2], hw)]
            recv_mp(part, dsem_s.at[c - 1, 1], dsem_r.at[c - 1, 1], 2)
            send_mp(part, part, dsem_s.at[c - 1, 2], dsem_r.at[c - 1, 2], 1)
    for c in range(chunks):
        if c == chunks - 1:
            part = oagd.at[grid_rows(c), cols(peer[2], hw)]
            recv_mp(part, dsem_s.at[c, 1], dsem_r.at[c, 1], 2)
            send_mp(part, part, dsem_s.at[c, 2], dsem_r.at[c, 2], 1)
        for r in (1, 3):
            recv_mp(oagd.at[grid_rows(c), cols(peer[r], hw)], dsem_s.at[c, r - 1], dsem_r.at[c, r - 1], r)
        change = dot_nn(oagd[grid_rows(c), :], wolast[...])
        whole = gfull[grid_rows(c), cols(m, feat)].astype(F32) + change
        for b in range(cb):
            ok = row_in_block < count_ref[node * gb + c * cb + b]
            piece = jnp.where(ok, whole[b * BLOCK:(b + 1) * BLOCK, :], 0.0)
            gout_ref[pl.ds((c * cb + b) * BLOCK, BLOCK), :] = piece.astype(BF16)

    for c in pending:
        c.wait_send()
    for slot in remote_slots:
        @pl.when(exists(slot - REACH))
        def _(slot=slot):
            for c in q_copies(slot) + o_copies(slot):
                c.wait_send()
            for l in range(layers - 1):
                for b in range(mb):
                    kv_copy(l, slot, b).wait_send()


def per_device(n_nodes, n_mp, grid_in, mesh_in, w_query, w_key, w_value, w_out, norm_gains,
               enc_list, proc_list, dec_list, grid_count):
    rows_g, feat = grid_in.shape
    rows_m = mesh_in.shape[0]
    width = feat * n_mp
    layers, _, hw = w_query.shape
    heads = hw // HEAD_DIM
    gb, mb = rows_g // BLOCK, rows_m // BLOCK
    chunks = gb // 2 if gb % 2 == 0 else gb
    chunk = rows_g // chunks
    norm_rows = max(chunk, rows_m)
    dma = lambda *shape: pltpu.SemaphoreType.DMA(shape)
    vm = pltpu.VMEM
    scratch = [
        vm((rows_g, width), BF16),
        vm((rows_m, width), BF16),
        vm((layers, width, 3 * hw), BF16),
        vm((layers - 1, hw * n_mp, width), BF16),
        vm((hw * n_mp, feat), BF16),
        vm((norm_rows, width), BF16),
        vm((norm_rows, width), BF16),
        vm((SLOTS, rows_m, hw), BF16),
        vm((2 * SLOTS, gb, rows_m), F32),
        vm((rows_g, hw), BF16),
        vm((hw, rows_g), BF16),
        vm((rows_g, hw), BF16),
        vm((SLOTS, hw, rows_m), BF16),
        vm((SLOTS, hw, rows_m), F32),
        vm((SLOTS, max(8, 2 * heads), rows_m), F32),
        vm((SLOTS, hw, rows_m), BF16),
        vm((SLOTS, max(8, 2 * heads), rows_m), F32),
        [vm((SLOTS * mb, 2, BLOCK, hw), BF16) for _ in range(layers - 1)],
        vm((layers - 1, rows_m, hw * n_mp), BF16),
        vm((rows_g, hw * n_mp), BF16),
        dma(8), dma(3), dma(3), dma(chunks, 3), dma(chunks, 3),
        dma(layers - 1, 3), dma(layers - 1, 3), dma(3), dma(3),
        dma(SLOTS), dma(SLOTS), dma(SLOTS), dma(SLOTS), dma(SLOTS), dma(SLOTS), dma(SLOTS), dma(SLOTS),
        dma(layers - 1, SLOTS, mb), dma(layers - 1, SLOTS, mb), dma(layers - 1, mb, 3), dma(layers - 1, mb, 3),
        dma(chunks, 3), dma(chunks, 3),
    ]
    smem = pl.BlockSpec(memory_space=pltpu.SMEM)
    anyspace = pl.BlockSpec(memory_space=pl.ANY)
    vmem = pl.BlockSpec(memory_space=pltpu.VMEM)
    return pl.pallas_call(
        functools.partial(kernel, (n_nodes, n_mp, chunks)),
        out_shape=(
            jax.ShapeDtypeStruct(grid_in.shape, BF16),
            jax.ShapeDtypeStruct(mesh_in.shape, BF16),
        ),
        in_specs=[smem] * 4 + [anyspace] * 6 + [vmem],
        out_specs=(vmem, vmem),
        scratch_shapes=scratch,
        compiler_params=pltpu.CompilerParams(
            collective_id=0, has_side_effects=True, vmem_limit_bytes=60 * 1024 * 1024
        ),
    )(enc_list, proc_list, dec_list, grid_count, grid_in, mesh_in, w_query, w_key, w_value, w_out, norm_gains)


def solution(mesh):
    placed = (
        P("nodes", "mp"),
        P("nodes", "mp"),
        P(None, None, "mp"),
        P(None, None, "mp"),
        P(None, None, "mp"),
        P(None, "mp", None),
        P(),
        P("nodes", None),
        P("nodes", None),
        P("nodes", None),
        P(),
    )
    return jax.shard_map(
        functools.partial(per_device, mesh.shape["nodes"], mesh.shape["mp"]),
        mesh=mesh,
        in_specs=placed,
        out_specs=(P("nodes", "mp"), P("nodes", "mp")),
        check_vma=False,
    )
```
